256 devices in a mesh: dp: 8 (over y, core), ctx: 32 (over z, x).
Axes of the slice: x: 4, y: 4, z: 8, core: 2. Of those that a mesh axis runs over, the one named last changes fastest.
Arguments:
- normed_hidden_input: bfloat16 [8, 4096, 4096], P('dp', 'ctx'), may hold values from -6 to 6
- frozen_query_projection: bfloat16 [8, 4096, 4096], P('dp', 'ctx'), may hold values from -24 to 24
- frozen_key_projection: bfloat16 [8, 4096, 4096], P('dp', 'ctx'), may hold values from -24 to 24
- frozen_value_projection: bfloat16 [8, 4096, 4096], P('dp', 'ctx'), may hold values from -6 to 6
- cotangent: bfloat16 [8, 4096, 4096], P('dp', 'ctx'), may hold values from -0.119628906 to 0.119628906
- adapter_down_maps: bfloat16 [3, 4096, 16], replicated, may hold values from -0.09375 to 0.09375
- adapter_up_maps: bfloat16 [3, 16, 4096], replicated, may hold values from -1.5 to 1.5
- head_shift_mask: int32 [32], replicated, may hold values from 0 to 1, as said below
Outputs:
- context: bfloat16 [8, 4096, 4096], P('dp', 'ctx')
- grad_down: float32 [3, 4096, 16], replicated
- grad_up: float32 [3, 16, 4096], replicated
The draws below stay inside these ranges and needn't reach their ends.
Inputs may be any that keep to these rules, and one draw needn't show every extreme that they name: `head_shift_mask`: exactly half of the entries are 1, the rest 0; which heads are shifted varies.
All inputs are finite; a program needn't handle non-finite values.
Results may differ from the reference program's by a relative error of at most 0.02.
The reference program's roundings to bfloat16 on the way count: a program that leaves them out, or rounds other values in their place, can miss the bound.
Values may be sent and summed in bfloat16 or wider, within the bound.
A program may use at most 64 MiB of HBM per device.

```python
import math
import jax
import jax.numpy as jnp
from jax import lax

MODEL_DIMENSION = 4096
HEADS = 32
HEAD_DIM = 128
ADAPTER_RANK = 16
GROUP = 1024
SHIFT = 512
DOCS = 8
LEN = 4096


def draw_frozen_query_projection(key, part):
    field = jnp.clip(jax.random.normal(jax.random.fold_in(key, 1), (DOCS, LEN, MODEL_DIMENSION), jnp.float32), -6.0, 6.0)
    return field.astype(jnp.bfloat16)


def draw_frozen_key_projection(key, part):
    field = jnp.clip(jax.random.normal(jax.random.fold_in(key, 2), (DOCS, LEN, MODEL_DIMENSION), jnp.float32), -6.0, 6.0)
    return field.astype(jnp.bfloat16)


def draw_head_shift_mask(key, part):
    order = jax.random.permutation(jax.random.fold_in(key, 3), HEADS)
    return (order < HEADS // 2).astype(jnp.int32)


def steps_of(stream_key, extent, pieces, low, largest):
    def one(axis_at, parts):
        heights = jax.random.uniform(jax.random.fold_in(jax.random.fold_in(stream_key, 6), axis_at), (parts,), jnp.float32, low / len(pieces), largest / len(pieces))
        return jnp.repeat(jnp.exp(heights), extent[axis_at] // parts).reshape((-1,) + (1,) * (len(extent) - axis_at - 1))

    level = one(*pieces[0])
    for cut in pieces[1:]:
        level = level * one(*cut)
    return level


def normal_values(stream_key, extent, spread, most, cuts=(), kind=jnp.bfloat16):
    loudness = steps_of(stream_key, extent, cuts, -0.22, 0.18) if cuts else 1.0
    result = jax.random.normal(stream_key, extent, jnp.float32) * spread * loudness
    return jnp.minimum(jnp.maximum(result, -most), most).astype(kind)


def setup_inputs(seed: int = 0) -> dict:
    key_of = jax.random.split(jax.random.key(seed), 9)
    return {
        "normed_hidden_input": normal_values(key_of[0], (DOCS, LEN, MODEL_DIMENSION), 1.0, 6.0, ((0, 8), (1, 32))),
        "frozen_query_projection": draw_frozen_query_projection(jax.random.fold_in(key_of[8], 71), 0),
        "frozen_key_projection": draw_frozen_key_projection(jax.random.fold_in(key_of[8], 71), 0),
        "frozen_value_projection": normal_values(key_of[3], (DOCS, LEN, MODEL_DIMENSION), 1.0, 6.0, ((0, 8), (1, 32))),
        "cotangent": normal_values(key_of[4], (DOCS, LEN, MODEL_DIMENSION), 0.02, 0.119628906, ((0, 8), (1, 32))),
        "adapter_down_maps": normal_values(key_of[5], (3, MODEL_DIMENSION, ADAPTER_RANK), MODEL_DIMENSION ** -0.5, 0.09375),
        "adapter_up_maps": normal_values(key_of[6], (3, ADAPTER_RANK, MODEL_DIMENSION), ADAPTER_RANK ** -0.5, 1.5),
        "head_shift_mask": draw_head_shift_mask(jax.random.fold_in(key_of[8], 71), 0),
    }


adapter_scale = 0.25

def shift_heads(values, shift_flags, amount):
    rolled = jnp.roll(values, amount, axis=0)
    return jnp.where(shift_flags[None, :, None] == 1, rolled, values)

def group_block(segment_list):
    queries, key_rows, value_rows, grad_out = segment_list
    group_len = queries.shape[0]
    softmax_scale = 1.0 / math.sqrt(queries.shape[2])
    query_f = queries.astype(jnp.float32)
    key_f = key_rows.astype(jnp.float32)
    value_f = value_rows.astype(jnp.float32)
    grad_f = grad_out.astype(jnp.float32)
    scores = jnp.einsum('qhe,khe->hqk', query_f, key_f) * softmax_scale
    row_ids = lax.broadcasted_iota(jnp.int32, (group_len, group_len), 0)
    col_ids = lax.broadcasted_iota(jnp.int32, (group_len, group_len), 1)
    scores = jnp.where((col_ids <= row_ids)[None], scores, -1e+30)
    highest = lax.optimization_barrier(jnp.max(scores, axis=2, keepdims=True))
    exponent = jnp.exp(scores - highest)
    weights = exponent / lax.optimization_barrier(jnp.sum(exponent, axis=2, keepdims=True))
    weights_low = weights.astype(jnp.bfloat16)
    attended = jnp.einsum('hqk,khe->qhe', weights_low.astype(jnp.float32), value_f).astype(jnp.bfloat16)
    weight_grad = jnp.einsum('qhe,khe->hqk', grad_f, value_f)
    row_inner = lax.optimization_barrier(jnp.sum(grad_f * attended.astype(jnp.float32), axis=2))
    score_grad = weights * (weight_grad - jnp.transpose(row_inner)[:, :, None])
    score_low = score_grad.astype(jnp.bfloat16).astype(jnp.float32)
    query_grad = (jnp.einsum('hqk,khe->qhe', score_low, key_f) * softmax_scale).astype(jnp.bfloat16)
    key_grad = (jnp.einsum('hqk,qhe->khe', score_low, query_f) * softmax_scale).astype(jnp.bfloat16)
    value_grad = jnp.einsum('hqk,qhe->khe', weights_low.astype(jnp.float32), grad_f).astype(jnp.bfloat16)
    return (attended, query_grad, key_grad, value_grad)

def attend_heads(queries, key_rows, value_rows, grad_out, shift_flags):
    total, heads, depth = queries.shape
    groups = total // GROUP

    def regroup(array):
        return shift_heads(array, shift_flags, -SHIFT).reshape(groups, GROUP, heads, depth)
    results = lax.map(group_block, (regroup(queries), regroup(key_rows), regroup(value_rows), regroup(grad_out)))
    return tuple((shift_heads(output_part.reshape(total, heads, depth), shift_flags, SHIFT) for output_part in results))

def per_document_step(segment_list, adapter_down_maps, adapter_up_maps, head_shift_mask):
    hidden_rows, query_in, key_in, value_in, grad_ctx = segment_list
    reduced_rank_rows = jnp.einsum('vl,hlq->hvq', hidden_rows.astype(jnp.float32), adapter_down_maps.astype(jnp.float32)).astype(jnp.bfloat16)
    adapter_update = jnp.einsum('bsc,bci->bsi', reduced_rank_rows.astype(jnp.float32), adapter_up_maps.astype(jnp.float32))
    frozen_stack = jnp.stack([query_in, key_in, value_in]).astype(jnp.float32)
    projected_rows = (frozen_stack + adapter_scale * adapter_update).astype(jnp.bfloat16)
    head_view = projected_rows.reshape(3, LEN, HEADS, HEAD_DIM)
    grad_view = grad_ctx.reshape(LEN, HEADS, HEAD_DIM)
    attended, query_grad, key_grad, value_grad = attend_heads(head_view[0], head_view[1], head_view[2], grad_view, head_shift_mask)
    context = attended.reshape(LEN, MODEL_DIMENSION)
    projection_gradient = jnp.stack([query_grad, key_grad, value_grad]).reshape(3, LEN, MODEL_DIMENSION).astype(jnp.float32)
    up_portion = adapter_scale * jnp.einsum('xvq,xvh->xqh', reduced_rank_rows.astype(jnp.float32), projection_gradient)
    backward_rank_rows = jnp.einsum('efu,eau->efa', projection_gradient, adapter_up_maps.astype(jnp.float32)).astype(jnp.bfloat16)
    down_portion = adapter_scale * jnp.einsum('ow,noi->nwi', hidden_rows.astype(jnp.float32), backward_rank_rows.astype(jnp.float32))
    return (context, down_portion, up_portion)

def reference(normed_hidden_input, frozen_query_projection, frozen_key_projection, frozen_value_projection, cotangent, adapter_down_maps, adapter_up_maps, head_shift_mask):

    def one_document(segment_list):
        return per_document_step(segment_list, adapter_down_maps, adapter_up_maps, head_shift_mask)
    context, down_parts, up_parts = lax.map(one_document, (normed_hidden_input, frozen_query_projection, frozen_key_projection, frozen_value_projection, cotangent))
    return (context, lax.optimization_barrier(jnp.sum(down_parts, axis=0)), lax.optimization_barrier(jnp.sum(up_parts, axis=0)))
```

```python
import functools
import math

import jax
import jax.numpy as jnp
from jax import lax
from jax.experimental import pallas as pl
from jax.experimental.pallas import tpu as pltpu
from jax.sharding import PartitionSpec as P

MESH = pl.DeviceIdType.MESH
HEAD_DIM = 128
RANK = 16
MAPS = 3
HEADS = 32
TOKENS = 128
MEMBERS = 8
CTX = 32
QUERY_BLOCK = 256
GROUP = MEMBERS * TOKENS
adapter_scale = 0.25
SOFTMAX_SCALE = 1.0 / math.sqrt(HEAD_DIM)
LOG2E = 1.4426950408889634
OFFSETS = (1, 3, 2, 4, 5, 7, 6)

BF = jnp.bfloat16
F32 = jnp.float32
NT = (((1,), (1,)), ((), ()))


def dot(a, b):
    return jnp.dot(a, b, preferred_element_type=F32)


def dot_nt(a, b):
    return lax.dot_general(a, b, NT, preferred_element_type=F32)


def place(me, kind):
    shifted = lax.rem(me + CTX - 4 * kind, CTX)
    position = lax.rem(shifted, MEMBERS)
    return position, shifted - position + 4 * kind


def partner(position, offset):
    half = lax.rem(position // 4 + offset // 4, 2)
    return half * 4 + lax.rem(lax.rem(position, 4) + offset % 4, 4)


def project_kernel(
    perm_ref, hidden_ref, query_ref, key_ref, value_ref, grad_ref, down_ref, up_ref, send_ref, low_ref, own_up_ref, low_rows
):
    step = pl.program_id(0)
    chunk, half = step // 2, lax.rem(step, 2)
    me = lax.axis_index("ctx")

    @pl.when(step == 0)
    def _():
        low_t = dot_nt(down_ref[...], hidden_ref[...])
        low_ref[...] = low_t.astype(BF)
        low_rows[...] = jnp.transpose(low_t).astype(BF)

    def columns_of(place_in_order):
        return pl.ds(pl.multiple_of(perm_ref[place_in_order] * HEAD_DIM, HEAD_DIM), HEAD_DIM)

    low = low_rows[...]
    first = 16 * (chunk // 2) + lax.rem(chunk, 2)
    for i in range(MEMBERS // 2):
        columns = columns_of(first + 2 * (half * (MEMBERS // 2) + i))
        for m, base_ref in enumerate((query_ref, key_ref, value_ref)):
            update = dot(low[:, m * RANK:(m + 1) * RANK], up_ref[m * RANK:(m + 1) * RANK, columns])
            send_ref[0, i, m * TOKENS:(m + 1) * TOKENS, :] = (
                base_ref[:, columns].astype(F32) + adapter_scale * update
            ).astype(BF)
        send_ref[0, i, 3 * TOKENS:4 * TOKENS, :] = grad_ref[:, columns]
    position, _ = place(me, chunk // 2)
    own_up_ref[chunk] = up_ref[:, columns_of(first + 2 * position)]


def restore_kernel(inv_ref, by_order_ref, context_ref):
    for head in range(HEADS):
        context_ref[:, head * HEAD_DIM:(head + 1) * HEAD_DIM] = by_order_ref[inv_ref[head]]


def attention_kernel(
    send_buf, low_own, own_up, hidden_ref,
    ctx_recv, grad_down_ref, grad_up_ref,
    recv_buf, low_buf, ctx_send, rank_send, rank_recv,
    kt_buf, vt_buf, gt_buf, dqt_buf, dk_buf, dv_buf,
    send_sem, recv_sem, low_send_sem, low_recv_sem, ctx_send_sem, ctx_recv_sem, rank_send_sem, rank_recv_sem,
):
    dp = lax.axis_index("dp")
    me = lax.axis_index("ctx")
    z, x = me // 4, lax.rem(me, 4)

    barrier = pltpu.get_barrier_semaphore()
    for dz in (-1, 0, 1):
        for dx in range(4):
            if dz == 0 and dx == 0:
                continue
            peer = lax.rem(z + dz + 8, 8) * 4 + lax.rem(x + dx, 4)
            pl.semaphore_signal(barrier, inc=1, device_id=(dp, peer), device_id_type=MESH)
    pl.semaphore_wait(barrier, 11)

    def low_copy(kind, offset):
        position, base = place(me, kind)
        target = partner(position, offset)
        return pltpu.make_async_remote_copy(
            src_ref=low_own, dst_ref=low_buf.at[kind, position],
            send_sem=low_send_sem.at[kind, offset], recv_sem=low_recv_sem.at[kind, offset],
            device_id=(dp, lax.rem(base + target, CTX)), device_id_type=MESH,
        )

    def data_copy(chunk, offset):
        position, base = place(me, chunk // 2)
        target = partner(position, offset)
        return pltpu.make_async_remote_copy(
            src_ref=send_buf.at[chunk, target], dst_ref=recv_buf.at[chunk, position],
            send_sem=send_sem.at[chunk, offset], recv_sem=recv_sem.at[chunk, offset],
            device_id=(dp, lax.rem(base + target, CTX)), device_id_type=MESH,
        )

    def context_copy(chunk, offset):
        kind = chunk // 2
        position, base = place(me, kind)
        target = partner(position, offset)
        return pltpu.make_async_remote_copy(
            src_ref=ctx_send.at[chunk, target],
            dst_ref=ctx_recv.at[16 * kind + 2 * position + lax.rem(chunk, 2)],
            send_sem=ctx_send_sem.at[chunk, offset], recv_sem=ctx_recv_sem.at[chunk, offset],
            device_id=(dp, lax.rem(base + target, CTX)), device_id_type=MESH,
        )

    def rank_copy(kind, offset):
        position, base = place(me, kind)
        target = partner(position, offset)
        return pltpu.make_async_remote_copy(
            src_ref=rank_send.at[kind, target], dst_ref=rank_recv.at[kind, offset],
            send_sem=rank_send_sem.at[kind, offset], recv_sem=rank_recv_sem.at[kind, offset],
            device_id=(dp, lax.rem(base + target, CTX)), device_id_type=MESH,
        )

    def own_copy(chunk):
        position, _ = place(me, chunk // 2)
        return pltpu.make_async_copy(
            send_buf.at[chunk, position], recv_buf.at[chunk, position], recv_sem.at[chunk, 0]
        )

    def start(chunk, carry):
        for offset in OFFSETS:
            data_copy(chunk, offset).start()
        own_copy(chunk).start()
        return carry

    start(0, 0)
    for kind in range(2):
        position, _ = place(me, kind)
        low_buf[kind, position] = low_own[...]
        for offset in OFFSETS:
            low_copy(kind, offset).start()
    lax.fori_loop(1, 4, start, 0)
    rank_send[...] = jnp.zeros_like(rank_send)
    for kind in range(2):
        for offset in OFFSETS:
            low_copy(kind, offset).wait_recv()

    def attend(chunk, carry):
        kind = chunk // 2
        position, _ = place(me, kind)
        for offset in OFFSETS:
            data_copy(chunk, offset).wait_recv()
        own_copy(chunk).wait()

        def rows(array, first, count):
            part = recv_buf[chunk, first // TOKENS:(first + count) // TOKENS, array * TOKENS:(array + 1) * TOKENS, :]
            return part.reshape(count, HEAD_DIM)

        kt_buf[...] = jnp.transpose(rows(1, 0, GROUP))
        vt_buf[...] = jnp.transpose(rows(2, 0, GROUP))
        gt_buf[...] = jnp.transpose(rows(3, 0, GROUP))
        for block in reversed(range(GROUP // QUERY_BLOCK)):
            first = block * QUERY_BLOCK
            seen = first + QUERY_BLOCK
            queries = rows(0, first, QUERY_BLOCK)
            grads = rows(3, first, QUERY_BLOCK)
            keys = rows(1, 0, seen)
            values = rows(2, 0, seen)
            scores = dot_nt(keys, queries)
            key_ids = lax.broadcasted_iota(jnp.int32, (seen, QUERY_BLOCK), 0)
            query_ids = lax.broadcasted_iota(jnp.int32, (seen, QUERY_BLOCK), 1) + first
            scores = jnp.where(key_ids <= query_ids, scores, -1e30)
            highest = jnp.max(scores, axis=0, keepdims=True)
            exponent = jnp.exp2((scores - highest) * (SOFTMAX_SCALE * LOG2E))
            weights = exponent * (1.0 / jnp.sum(exponent, axis=0, keepdims=True))
            weights_low = weights.astype(BF)
            attended = dot(vt_buf[:, :seen], weights_low).astype(BF).astype(F32)
            weight_grad = dot_nt(values, grads)
            row_inner = jnp.sum(gt_buf[:, first:seen].astype(F32) * attended, axis=0, keepdims=True)
            score_low = (weights * (weight_grad - row_inner)).astype(BF)
            dqt_buf[:, first:seen] = (dot(kt_buf[:, :seen], score_low) * SOFTMAX_SCALE).astype(BF)
            dk = dot(score_low, queries)
            dv = dot(weights_low, grads)
            if seen == GROUP:
                dk_buf[...] = dk
                dv_buf[...] = dv
            else:
                dk_buf[:seen] += dk
                dv_buf[:seen] += dv
            out_rows = jnp.transpose(attended).astype(BF).reshape(QUERY_BLOCK // TOKENS, TOKENS, HEAD_DIM)
            ctx_send[chunk, first // TOKENS:seen // TOKENS] = out_rows
        for offset in OFFSETS:
            context_copy(chunk, offset).start()
        own = 16 * kind + 2 * position + lax.rem(chunk, 2)
        ctx_recv[own] = ctx_send[chunk, position]

        dqt = dqt_buf[...]
        dk = (dk_buf[...] * SOFTMAX_SCALE).astype(BF)
        dv = dv_buf[...].astype(BF)
        low_all = jnp.concatenate([low_buf[kind, s] for s in range(MEMBERS)], axis=1)
        up = own_up[chunk]
        grad_up_ref[chunk] = adapter_scale * jnp.concatenate(
            [dot_nt(low_all[0:16], dqt), dot(low_all[16:32], dk), dot(low_all[32:48], dv)], axis=0
        )
        ranks = jnp.concatenate([dot(up[0:16], dqt), dot_nt(up[16:32], dk), dot_nt(up[32:48], dv)], axis=0)
        for s in range(MEMBERS):
            rank_send[kind, s] += ranks[:, s * TOKENS:(s + 1) * TOKENS]

        @pl.when(lax.rem(chunk, 2) == 1)
        def _():
            for offset in OFFSETS:
                rank_copy(kind, offset).start()

        return carry

    lax.fori_loop(0, 4, attend, 0)

    for kind in range(2):
        for offset in OFFSETS:
            rank_copy(kind, offset).wait_recv()
    total = jnp.zeros((MAPS * RANK, TOKENS), F32)
    for kind in range(2):
        position, _ = place(me, kind)
        total += rank_send[kind, position]
        for offset in OFFSETS:
            total += rank_recv[kind, offset]
    grad_down_ref[...] = adapter_scale * dot(total.astype(BF), hidden_ref[...])

    def finish(chunk, carry):
        for offset in OFFSETS:
            context_copy(chunk, offset).wait_recv()
            context_copy(chunk, offset).wait_send()
            data_copy(chunk, offset).wait_send()
        return carry

    lax.fori_loop(0, 4, finish, 0)
    for kind in range(2):
        for offset in OFFSETS:
            low_copy(kind, offset).wait_send()
            rank_copy(kind, offset).wait_send()


def body(hidden, query, key, value, cotangent, down, up, mask):
    width = hidden.shape[2]
    order = jnp.arange(HEADS, dtype=jnp.int32)
    shifted = (mask == 1).astype(jnp.int32)
    ahead = (order[None, :] < order[:, None]).astype(jnp.int32)
    shifted_ahead = jnp.sum(ahead * shifted[None, :], axis=1)
    inverse = jnp.where(shifted == 1, HEADS // 2 + shifted_ahead, order - shifted_ahead)
    perm = jnp.sum(jnp.where(inverse[None, :] == order[:, None], order[None, :], 0), axis=1)

    vmem = pl.BlockSpec(memory_space=pltpu.VMEM)
    smem = pl.BlockSpec(memory_space=pltpu.SMEM)
    dma = pltpu.SemaphoreType.DMA
    any_space = pl.BlockSpec(memory_space=pl.ANY)
    whole = pl.BlockSpec((TOKENS, width), lambda i, p: (0, 0))
    maps = pl.BlockSpec((MAPS * RANK, width), lambda i, p: (0, 0))
    send, low_t, own_up = pl.pallas_call(
        project_kernel,
        grid_spec=pltpu.PrefetchScalarGridSpec(
            num_scalar_prefetch=1,
            grid=(8,),
            in_specs=[whole] * 5 + [maps] * 2,
            out_specs=(
                pl.BlockSpec((1, MEMBERS // 2, 4 * TOKENS, HEAD_DIM), lambda i, p: (i // 2, i % 2, 0, 0)),
                pl.BlockSpec((MAPS * RANK, TOKENS), lambda i, p: (0, 0)),
                pl.BlockSpec((4, MAPS * RANK, HEAD_DIM), lambda i, p: (0, 0, 0)),
            ),
            scratch_shapes=[pltpu.VMEM((TOKENS, MAPS * RANK), BF)],
        ),
        out_shape=(
            jax.ShapeDtypeStruct((4, MEMBERS, 4 * TOKENS, HEAD_DIM), BF),
            jax.ShapeDtypeStruct((MAPS * RANK, TOKENS), BF),
            jax.ShapeDtypeStruct((4, MAPS * RANK, HEAD_DIM), BF),
        ),
        compiler_params=pltpu.CompilerParams(vmem_limit_bytes=32 * 1024 * 1024),
        name="project",
    )(
        perm, hidden[0], query[0], key[0], value[0], cotangent[0],
        jnp.transpose(down, (0, 2, 1)).reshape(MAPS * RANK, width), up.reshape(MAPS * RANK, width),
    )
    by_order, grad_down, grad_up = pl.pallas_call(
        attention_kernel,
        out_shape=(
            jax.ShapeDtypeStruct((HEADS, TOKENS, HEAD_DIM), BF),
            jax.ShapeDtypeStruct((MAPS * RANK, width), F32),
            jax.ShapeDtypeStruct((4, MAPS * RANK, HEAD_DIM), F32),
        ),
        in_specs=[any_space, vmem, vmem, vmem],
        out_specs=(vmem, vmem, vmem),
        scratch_shapes=[
            pltpu.VMEM((4, MEMBERS, 4 * TOKENS, HEAD_DIM), BF),
            pltpu.VMEM((2, MEMBERS, MAPS * RANK, TOKENS), BF),
            pltpu.VMEM((4, MEMBERS, TOKENS, HEAD_DIM), BF),
            pltpu.VMEM((2, MEMBERS, MAPS * RANK, TOKENS), F32),
            pltpu.VMEM((2, MEMBERS, MAPS * RANK, TOKENS), F32),
            pltpu.VMEM((HEAD_DIM, GROUP), BF),
            pltpu.VMEM((HEAD_DIM, GROUP), BF),
            pltpu.VMEM((HEAD_DIM, GROUP), BF),
            pltpu.VMEM((HEAD_DIM, GROUP), BF),
            pltpu.VMEM((GROUP, HEAD_DIM), F32),
            pltpu.VMEM((GROUP, HEAD_DIM), F32),
            dma((4, MEMBERS)), dma((4, MEMBERS)), dma((2, MEMBERS)), dma((2, MEMBERS)),
            dma((4, MEMBERS)), dma((4, MEMBERS)), dma((2, MEMBERS)), dma((2, MEMBERS)),
        ],
        compiler_params=pltpu.CompilerParams(
            collective_id=0, has_side_effects=True, vmem_limit_bytes=40 * 1024 * 1024
        ),
        name="shifted_group_attention",
    )(send, low_t, own_up, hidden[0])
    context = pl.pallas_call(
        restore_kernel,
        out_shape=jax.ShapeDtypeStruct((TOKENS, width), BF),
        in_specs=[smem, vmem],
        out_specs=vmem,
        name="restore_heads",
    )(inverse, by_order)

    me = lax.axis_index("ctx")
    plain, _ = place(me, 0)
    moved, _ = place(me, 1)
    by_head = jnp.zeros((HEADS, MAPS * RANK, HEAD_DIM), F32)
    by_head = lax.dynamic_update_slice_in_dim(by_head, grad_up[0:2], 2 * plain, 0)
    by_head = lax.dynamic_update_slice_in_dim(by_head, grad_up[2:4], 16 + 2 * moved, 0)
    grad_down, by_head = lax.psum((grad_down, by_head), ("dp", "ctx"))
    grad_up = jnp.transpose(jnp.take(by_head, inverse, axis=0), (1, 0, 2)).reshape(MAPS, RANK, width)
    grad_down = jnp.transpose(grad_down.reshape(MAPS, RANK, width), (0, 2, 1))
    return context[None], grad_down, grad_up


def solution(mesh):
    placed = (P("dp", "ctx", None),) * 5 + (P(),) * 3
    return jax.shard_map(
        body, mesh=mesh, in_specs=placed, out_specs=(P("dp", "ctx", None), P(), P()), check_vma=False
    )
```

```python
import functools
import math

import jax
import jax.numpy as jnp
from jax import lax
from jax.experimental import pallas as pl
from jax.experimental.pallas import tpu as pltpu
from jax.sharding import PartitionSpec as P

MESH = pl.DeviceIdType.MESH
HEAD_DIM = 128
RANK = 16
MAPS = 3
HEADS = 32
TOKENS = 128
MEMBERS = 8
CTX = 32
QUERY_BLOCK = 256
GROUP = MEMBERS * TOKENS
adapter_scale = 0.25
SOFTMAX_SCALE = 1.0 / math.sqrt(HEAD_DIM)
LOG2E = 1.4426950408889634
OFFSETS = (1, 3, 2, 4, 5, 7, 6)

HALF = MAPS * RANK // 2
PIECES = 16
PIECE = 256
PAIR_PARTS = 4
PAIR_PIECES = PIECES // PAIR_PARTS

BF = jnp.bfloat16
F32 = jnp.float32
NT = (((1,), (1,)), ((), ()))


def dot(a, b):
    return jnp.dot(a, b, preferred_element_type=F32)


def dot_nt(a, b):
    return lax.dot_general(a, b, NT, preferred_element_type=F32)


def place(me, kind):
    shifted = lax.rem(me + CTX - 4 * kind, CTX)
    position = lax.rem(shifted, MEMBERS)
    return position, shifted - position + 4 * kind


def partner(position, offset):
    half = lax.rem(position // 4 + offset // 4, 2)
    return half * 4 + lax.rem(lax.rem(position, 4) + offset % 4, 4)


def project_kernel(
    perm_ref, hidden_ref, query_ref, key_ref, value_ref, grad_ref, down_ref, up_ref, send_ref, low_ref, own_up_ref, low_rows
):
    step = pl.program_id(0)
    chunk, half = step // 2, lax.rem(step, 2)
    me = lax.axis_index("ctx")

    @pl.when(step == 0)
    def _():
        low_t = dot_nt(down_ref[...], hidden_ref[...])
        low_ref[...] = low_t.astype(BF)
        low_rows[...] = jnp.transpose(low_t).astype(BF)

    def columns_of(place_in_order):
        return pl.ds(pl.multiple_of(perm_ref[place_in_order] * HEAD_DIM, HEAD_DIM), HEAD_DIM)

    low = low_rows[...]
    first = 16 * (chunk // 2) + lax.rem(chunk, 2)
    for i in range(MEMBERS // 2):
        columns = columns_of(first + 2 * (half * (MEMBERS // 2) + i))
        for m, base_ref in enumerate((query_ref, key_ref, value_ref)):
            update = dot(low[:, m * RANK:(m + 1) * RANK], up_ref[m * RANK:(m + 1) * RANK, columns])
            send_ref[0, i, m * TOKENS:(m + 1) * TOKENS, :] = (
                base_ref[:, columns].astype(F32) + adapter_scale * update
            ).astype(BF)
        send_ref[0, i, 3 * TOKENS:4 * TOKENS, :] = grad_ref[:, columns]
    position, _ = place(me, chunk // 2)
    own_up_ref[chunk] = up_ref[:, columns_of(first + 2 * position)]


def restore_kernel(inv_ref, by_order_ref, up_by_order_ref, context_ref, grad_up_ref):
    for head in range(HEADS):
        context_ref[:, head * HEAD_DIM:(head + 1) * HEAD_DIM] = by_order_ref[inv_ref[head]]
        grad_up_ref[:, head * HEAD_DIM:(head + 1) * HEAD_DIM] = up_by_order_ref[inv_ref[head]]


def attention_kernel(
    send_buf, low_own, own_up, hidden_ref,
    ctx_recv, grad_down_ref, grad_up_ref,
    recv_buf, low_buf, ctx_send, rank_send, rank_recv,
    kt_buf, vt_buf, gt_buf, dqt_buf, dk_buf, dv_buf,
    down_part, down_pair, down_sum, down_recv, up_part, up_pair, up_sum, up_recv, line_buf, all_buf,
    send_sem, recv_sem, low_send_sem, low_recv_sem, ctx_send_sem, ctx_recv_sem, rank_send_sem, rank_recv_sem,
    pair_send_sem, pair_recv_sem, plane_send_sem, plane_recv_sem, side_send_sem, side_recv_sem,
    line_send_sem, line_recv_sem, all_send_sem, all_recv_sem, last_send_sem, last_recv_sem,
):
    dp = lax.axis_index("dp")
    me = lax.axis_index("ctx")
    z, x = me // 4, lax.rem(me, 4)
    y, core = dp // 2, lax.rem(dp, 2)
    own_piece = y * 4 + x

    barrier = pltpu.get_barrier_semaphore()
    for dz in (-1, 0, 1):
        for dx in range(4):
            if dz == 0 and dx == 0:
                continue
            peer = lax.rem(z + dz + 8, 8) * 4 + lax.rem(x + dx, 4)
            pl.semaphore_signal(barrier, inc=1, device_id=(dp, peer), device_id_type=MESH)
    for dz in range(2, 7):
        pl.semaphore_signal(barrier, inc=1, device_id=(dp, lax.rem(z + dz, 8) * 4 + x), device_id_type=MESH)
    for dy in range(1, 4):
        for dx in range(4):
            peer = (lax.rem(y + dy, 4) * 2 + core, z * 4 + lax.rem(x + dx, 4))
            pl.semaphore_signal(barrier, inc=1, device_id=peer, device_id_type=MESH)
    sibling = (y * 2 + 1 - core, me)
    pl.semaphore_signal(barrier, inc=1, device_id=sibling, device_id_type=MESH)
    pl.semaphore_wait(barrier, 29)

    def low_copy(kind, offset):
        position, base = place(me, kind)
        target = partner(position, offset)
        return pltpu.make_async_remote_copy(
            src_ref=low_own, dst_ref=low_buf.at[kind, position],
            send_sem=low_send_sem.at[kind, offset], recv_sem=low_recv_sem.at[kind, offset],
            device_id=(dp, lax.rem(base + target, CTX)), device_id_type=MESH,
        )

    def data_copy(chunk, offset):
        position, base = place(me, chunk // 2)
        target = partner(position, offset)
        return pltpu.make_async_remote_copy(
            src_ref=send_buf.at[chunk, target], dst_ref=recv_buf.at[chunk, position],
            send_sem=send_sem.at[chunk, offset], recv_sem=recv_sem.at[chunk, offset],
            device_id=(dp, lax.rem(base + target, CTX)), device_id_type=MESH,
        )

    def context_copy(chunk, offset):
        kind = chunk // 2
        position, base = place(me, kind)
        target = partner(position, offset)
        return pltpu.make_async_remote_copy(
            src_ref=ctx_send.at[chunk, target],
            dst_ref=ctx_recv.at[16 * kind + 2 * position + lax.rem(chunk, 2)],
            send_sem=ctx_send_sem.at[chunk, offset], recv_sem=ctx_recv_sem.at[chunk, offset],
            device_id=(dp, lax.rem(base + target, CTX)), device_id_type=MESH,
        )

    def rank_copy(kind, offset):
        position, base = place(me, kind)
        target = partner(position, offset)
        return pltpu.make_async_remote_copy(
            src_ref=rank_send.at[kind, target], dst_ref=rank_recv.at[kind, offset],
            send_sem=rank_send_sem.at[kind, offset], recv_sem=rank_recv_sem.at[kind, offset],
            device_id=(dp, lax.rem(base + target, CTX)), device_id_type=MESH,
        )

    def own_copy(chunk):
        position, _ = place(me, chunk // 2)
        return pltpu.make_async_copy(
            send_buf.at[chunk, position], recv_buf.at[chunk, position], recv_sem.at[chunk, 0]
        )

    def start(chunk, carry):
        for offset in OFFSETS:
            data_copy(chunk, offset).start()
        own_copy(chunk).start()
        return carry

    start(0, 0)
    for kind in range(2):
        position, _ = place(me, kind)
        low_buf[kind, position] = low_own[...]
        for offset in OFFSETS:
            low_copy(kind, offset).start()
    lax.fori_loop(1, 4, start, 0)
    rank_send[...] = jnp.zeros_like(rank_send)
    for kind in range(2):
        for offset in OFFSETS:
            low_copy(kind, offset).wait_recv()

    def attend(chunk, carry):
        kind = chunk // 2
        position, _ = place(me, kind)
        for offset in OFFSETS:
            data_copy(chunk, offset).wait_recv()
        own_copy(chunk).wait()

        def rows(array, first, count):
            part = recv_buf[chunk, first // TOKENS:(first + count) // TOKENS, array * TOKENS:(array + 1) * TOKENS, :]
            return part.reshape(count, HEAD_DIM)

        kt_buf[...] = jnp.transpose(rows(1, 0, GROUP))
        vt_buf[...] = jnp.transpose(rows(2, 0, GROUP))
        gt_buf[...] = jnp.transpose(rows(3, 0, GROUP))
        for block in reversed(range(GROUP // QUERY_BLOCK)):
            first = block * QUERY_BLOCK
            seen = first + QUERY_BLOCK
            queries = rows(0, first, QUERY_BLOCK)
            grads = rows(3, first, QUERY_BLOCK)
            keys = rows(1, 0, seen)
            values = rows(2, 0, seen)
            scores = dot_nt(keys, queries)
            key_ids = lax.broadcasted_iota(jnp.int32, (seen, QUERY_BLOCK), 0)
            query_ids = lax.broadcasted_iota(jnp.int32, (seen, QUERY_BLOCK), 1) + first
            scores = jnp.where(key_ids <= query_ids, scores, -1e30)
            highest = jnp.max(scores, axis=0, keepdims=True)
            exponent = jnp.exp2((scores - highest) * (SOFTMAX_SCALE * LOG2E))
            weights = exponent * (1.0 / jnp.sum(exponent, axis=0, keepdims=True))
            weights_low = weights.astype(BF)
            attended = dot(vt_buf[:, :seen], weights_low).astype(BF).astype(F32)
            weight_grad = dot_nt(values, grads)
            row_inner = jnp.sum(gt_buf[:, first:seen].astype(F32) * attended, axis=0, keepdims=True)
            score_low = (weights * (weight_grad - row_inner)).astype(BF)
            dqt_buf[:, first:seen] = (dot(kt_buf[:, :seen], score_low) * SOFTMAX_SCALE).astype(BF)
            dk = dot(score_low, queries)
            dv = dot(weights_low, grads)
            if seen == GROUP:
                dk_buf[...] = dk
                dv_buf[...] = dv
            else:
                dk_buf[:seen] += dk
                dv_buf[:seen] += dv
            out_rows = jnp.transpose(attended).astype(BF).reshape(QUERY_BLOCK // TOKENS, TOKENS, HEAD_DIM)
            ctx_send[chunk, first // TOKENS:seen // TOKENS] = out_rows
        for offset in OFFSETS:
            context_copy(chunk, offset).start()
        own = 16 * kind + 2 * position + lax.rem(chunk, 2)
        ctx_recv[own] = ctx_send[chunk, position]

        dqt = dqt_buf[...]
        dk = (dk_buf[...] * SOFTMAX_SCALE).astype(BF)
        dv = dv_buf[...].astype(BF)
        low_all = jnp.concatenate([low_buf[kind, s] for s in range(MEMBERS)], axis=1)
        up = own_up[chunk]
        up_grad = adapter_scale * jnp.concatenate(
            [dot_nt(low_all[0:16], dqt), dot(low_all[16:32], dk), dot(low_all[32:48], dv)], axis=0
        )
        up_part[0, chunk] = up_grad[:HALF]
        up_part[1, chunk] = up_grad[HALF:]
        ranks = jnp.concatenate([dot(up[0:16], dqt), dot_nt(up[16:32], dk), dot_nt(up[32:48], dv)], axis=0)
        for s in range(MEMBERS):
            rank_send[kind, s] += ranks[:, s * TOKENS:(s + 1) * TOKENS]

        @pl.when(lax.rem(chunk, 2) == 1)
        def _():
            for offset in OFFSETS:
                rank_copy(kind, offset).start()

        return carry

    lax.fori_loop(0, 4, attend, 0)

    for kind in range(2):
        for offset in OFFSETS:
            rank_copy(kind, offset).wait_recv()
    total = jnp.zeros((MAPS * RANK, TOKENS), F32)
    for kind in range(2):
        position, _ = place(me, kind)
        total += rank_send[kind, position]
        for offset in OFFSETS:
            total += rank_recv[kind, offset]
    total_low = total.astype(BF)

    def pair_copy(part):
        if part == PAIR_PARTS:
            source, target = up_part.at[1 - core], up_pair
        else:
            span = pl.ds(part * PAIR_PIECES, PAIR_PIECES)
            source, target = down_part.at[1 - core, span], down_pair.at[span]
        return pltpu.make_async_remote_copy(
            src_ref=source, dst_ref=target, send_sem=pair_send_sem.at[part], recv_sem=pair_recv_sem.at[part],
            device_id=sibling, device_id_type=MESH,
        )

    def plane_device(offset):
        to_y, to_x = lax.rem(y + offset // 4, 4), lax.rem(x + offset % 4, 4)
        return to_y * 4 + to_x, (to_y * 2 + core, z * 4 + to_x)

    def plane_copy(offset):
        piece, device = plane_device(offset)
        return pltpu.make_async_remote_copy(
            src_ref=down_sum.at[piece], dst_ref=down_recv.at[offset],
            send_sem=plane_send_sem.at[offset], recv_sem=plane_recv_sem.at[offset],
            device_id=device, device_id_type=MESH,
        )

    def side_copy(offset):
        to_y = lax.rem(y + offset, 4)
        return pltpu.make_async_remote_copy(
            src_ref=up_sum.at[to_y], dst_ref=up_recv.at[offset],
            send_sem=side_send_sem.at[offset], recv_sem=side_recv_sem.at[offset],
            device_id=(to_y * 2 + core, me), device_id_type=MESH,
        )

    def line_copy(offset):
        return pltpu.make_async_remote_copy(
            src_ref=line_buf.at[z], dst_ref=line_buf.at[z],
            send_sem=line_send_sem.at[offset], recv_sem=line_recv_sem.at[offset],
            device_id=(dp, lax.rem(z + offset, 8) * 4 + x), device_id_type=MESH,
        )

    def all_copy(offset):
        _, device = plane_device(offset)
        return pltpu.make_async_remote_copy(
            src_ref=all_buf.at[core, own_piece], dst_ref=all_buf.at[core, own_piece],
            send_sem=all_send_sem.at[offset], recv_sem=all_recv_sem.at[offset],
            device_id=device, device_id_type=MESH,
        )

    def last_copy(offset):
        piece = lax.rem(y + 4 - offset // 4, 4) * 4 + lax.rem(x + 4 - offset % 4, 4)
        return pltpu.make_async_remote_copy(
            src_ref=all_buf.at[core, piece], dst_ref=all_buf.at[core, piece],
            send_sem=last_send_sem.at[offset], recv_sem=last_recv_sem.at[offset],
            device_id=sibling, device_id_type=MESH,
        )

    pair_copy(PAIR_PARTS).start()
    for part in range(PAIR_PARTS):
        for piece in range(part * PAIR_PIECES, (part + 1) * PAIR_PIECES):
            grads = adapter_scale * dot(total_low, hidden_ref[:, piece * PIECE:(piece + 1) * PIECE])
            down_part[0, piece] = grads[:HALF]
            down_part[1, piece] = grads[HALF:]
        pair_copy(part).start()
    pair_copy(PAIR_PARTS).wait_recv()
    up_sum[...] = up_part[core] + up_pair[...]
    for offset in range(1, 4):
        side_copy(offset).start()
    for part in range(PAIR_PARTS):
        pair_copy(part).wait_recv()
    down_sum[...] = down_part[core] + down_pair[...]
    for offset in range(1, PIECES):
        plane_copy(offset).start()

    for offset in range(1, 4):
        side_copy(offset).wait_recv()
    line_buf[z, :, PIECE:] = ((up_sum[y] + up_recv[1]) + up_recv[2]) + up_recv[3]
    reduced = down_sum[own_piece]
    for offset in range(1, PIECES):
        plane_copy(offset).wait_recv()
        reduced = reduced + down_recv[offset]
    line_buf[z, :, :PIECE] = reduced
    for offset in range(1, 8):
        line_copy(offset).start()
    for offset in range(1, 8):
        line_copy(offset).wait_recv()
    even = line_buf[0] + line_buf[2] + (line_buf[4] + line_buf[6])
    odd = line_buf[1] + line_buf[3] + (line_buf[5] + line_buf[7])
    all_buf[core, own_piece, :, :PIECE] = even[:, :PIECE] + odd[:, :PIECE]
    all_buf[core, own_piece, :, PIECE:PIECE + HEAD_DIM] = even[:, PIECE:]
    all_buf[core, own_piece, :, PIECE + HEAD_DIM:] = odd[:, PIECE:]
    for offset in range(1, PIECES):
        all_copy(offset).start()
    last_copy(0).start()
    for offset in range(1, PIECES):
        all_copy(offset).wait_recv()
        last_copy(offset).start()
    for offset in range(PIECES):
        last_copy(offset).wait_recv()

    for half in range(2):
        for piece in range(PIECES):
            at_y, at_x = piece // 4, piece % 4
            rows_of = slice(half * HALF, (half + 1) * HALF)
            grad_down_ref[rows_of, piece * PIECE:(piece + 1) * PIECE] = all_buf[half, piece, :, :PIECE]
            for parity in range(2):
                position = (parity if at_y < 2 else 1 - parity) * 4 + at_x
                grad_up_ref[16 * (at_y // 2) + 2 * position + at_y % 2, rows_of] = all_buf[
                    half, piece, :, PIECE + parity * HEAD_DIM:PIECE + (parity + 1) * HEAD_DIM
                ]

    def finish(chunk, carry):
        for offset in OFFSETS:
            context_copy(chunk, offset).wait_recv()
            context_copy(chunk, offset).wait_send()
            data_copy(chunk, offset).wait_send()
        return carry

    lax.fori_loop(0, 4, finish, 0)
    for kind in range(2):
        for offset in OFFSETS:
            low_copy(kind, offset).wait_send()
            rank_copy(kind, offset).wait_send()
    for part in range(PAIR_PARTS + 1):
        pair_copy(part).wait_send()
    for offset in range(1, 4):
        side_copy(offset).wait_send()
    for offset in range(1, 8):
        line_copy(offset).wait_send()
    for offset in range(PIECES):
        last_copy(offset).wait_send()
        if offset:
            plane_copy(offset).wait_send()
            all_copy(offset).wait_send()


def body(hidden, query, key, value, cotangent, down, up, mask):
    width = hidden.shape[2]
    order = jnp.arange(HEADS, dtype=jnp.int32)
    shifted = (mask == 1).astype(jnp.int32)
    ahead = (order[None, :] < order[:, None]).astype(jnp.int32)
    shifted_ahead = jnp.sum(ahead * shifted[None, :], axis=1)
    inverse = jnp.where(shifted == 1, HEADS // 2 + shifted_ahead, order - shifted_ahead)
    perm = jnp.sum(jnp.where(inverse[None, :] == order[:, None], order[None, :], 0), axis=1)

    vmem = pl.BlockSpec(memory_space=pltpu.VMEM)
    smem = pl.BlockSpec(memory_space=pltpu.SMEM)
    dma = pltpu.SemaphoreType.DMA
    any_space = pl.BlockSpec(memory_space=pl.ANY)
    whole = pl.BlockSpec((TOKENS, width), lambda i, p: (0, 0))
    maps = pl.BlockSpec((MAPS * RANK, width), lambda i, p: (0, 0))
    send, low_t, own_up = pl.pallas_call(
        project_kernel,
        grid_spec=pltpu.PrefetchScalarGridSpec(
            num_scalar_prefetch=1,
            grid=(8,),
            in_specs=[whole] * 5 + [maps] * 2,
            out_specs=(
                pl.BlockSpec((1, MEMBERS // 2, 4 * TOKENS, HEAD_DIM), lambda i, p: (i // 2, i % 2, 0, 0)),
                pl.BlockSpec((MAPS * RANK, TOKENS), lambda i, p: (0, 0)),
                pl.BlockSpec((4, MAPS * RANK, HEAD_DIM), lambda i, p: (0, 0, 0)),
            ),
            scratch_shapes=[pltpu.VMEM((TOKENS, MAPS * RANK), BF)],
        ),
        out_shape=(
            jax.ShapeDtypeStruct((4, MEMBERS, 4 * TOKENS, HEAD_DIM), BF),
            jax.ShapeDtypeStruct((MAPS * RANK, TOKENS), BF),
            jax.ShapeDtypeStruct((4, MAPS * RANK, HEAD_DIM), BF),
        ),
        compiler_params=pltpu.CompilerParams(vmem_limit_bytes=32 * 1024 * 1024),
        name="project",
    )(
        perm, hidden[0], query[0], key[0], value[0], cotangent[0],
        jnp.transpose(down, (0, 2, 1)).reshape(MAPS * RANK, width), up.reshape(MAPS * RANK, width),
    )
    by_order, grad_down, grad_up = pl.pallas_call(
        attention_kernel,
        out_shape=(
            jax.ShapeDtypeStruct((HEADS, TOKENS, HEAD_DIM), BF),
            jax.ShapeDtypeStruct((MAPS * RANK, width), F32),
            jax.ShapeDtypeStruct((HEADS, MAPS * RANK, HEAD_DIM), F32),
        ),
        in_specs=[any_space, vmem, vmem, vmem],
        out_specs=(vmem, vmem, vmem),
        scratch_shapes=[
            pltpu.VMEM((4, MEMBERS, 4 * TOKENS, HEAD_DIM), BF),
            pltpu.VMEM((2, MEMBERS, MAPS * RANK, TOKENS), BF),
            pltpu.VMEM((4, MEMBERS, TOKENS, HEAD_DIM), BF),
            pltpu.VMEM((2, MEMBERS, MAPS * RANK, TOKENS), F32),
            pltpu.VMEM((2, MEMBERS, MAPS * RANK, TOKENS), F32),
            pltpu.VMEM((HEAD_DIM, GROUP), BF),
            pltpu.VMEM((HEAD_DIM, GROUP), BF),
            pltpu.VMEM((HEAD_DIM, GROUP), BF),
            pltpu.VMEM((HEAD_DIM, GROUP), BF),
            pltpu.VMEM((GROUP, HEAD_DIM), F32),
            pltpu.VMEM((GROUP, HEAD_DIM), F32),
            pltpu.VMEM((2, PIECES, HALF, PIECE), F32),
            pltpu.VMEM((PIECES, HALF, PIECE), F32),
            pltpu.VMEM((PIECES, HALF, PIECE), F32),
            pltpu.VMEM((PIECES, HALF, PIECE), F32),
            pltpu.VMEM((2, 4, HALF, HEAD_DIM), F32),
            pltpu.VMEM((4, HALF, HEAD_DIM), F32),
            pltpu.VMEM((4, HALF, HEAD_DIM), F32),
            pltpu.VMEM((4, HALF, HEAD_DIM), F32),
            pltpu.VMEM((8, HALF, PIECE + HEAD_DIM), F32),
            pltpu.VMEM((2, PIECES, HALF, PIECE + 2 * HEAD_DIM), F32),
            dma((4, MEMBERS)), dma((4, MEMBERS)), dma((2, MEMBERS)), dma((2, MEMBERS)),
            dma((4, MEMBERS)), dma((4, MEMBERS)), dma((2, MEMBERS)), dma((2, MEMBERS)),
            dma((PAIR_PARTS + 1,)), dma((PAIR_PARTS + 1,)), dma((PIECES,)), dma((PIECES,)), dma((4,)), dma((4,)),
            dma((8,)), dma((8,)), dma((PIECES,)), dma((PIECES,)), dma((PIECES,)), dma((PIECES,)),
        ],
        compiler_params=pltpu.CompilerParams(
            collective_id=0, has_side_effects=True, vmem_limit_bytes=40 * 1024 * 1024
        ),
        name="shifted_group_attention",
    )(send, low_t, own_up, hidden[0])
    context, grad_up = pl.pallas_call(
        restore_kernel,
        out_shape=(
            jax.ShapeDtypeStruct((TOKENS, width), BF),
            jax.ShapeDtypeStruct((MAPS * RANK, width), F32),
        ),
        in_specs=[smem, vmem, vmem],
        out_specs=(vmem, vmem),
        name="restore_heads",
    )(inverse, by_order, grad_up)
    grad_up = grad_up.reshape(MAPS, RANK, width)
    grad_down = jnp.transpose(grad_down.reshape(MAPS, RANK, width), (0, 2, 1))
    return context[None], grad_down, grad_up


def solution(mesh):
    placed = (P("dp", "ctx", None),) * 5 + (P(),) * 3
    return jax.shard_map(
        body, mesh=mesh, in_specs=placed, out_specs=(P("dp", "ctx", None), P(), P()), check_vma=False
    )
```

```python
import functools
import math

import jax
import jax.numpy as jnp
from jax import lax
from jax.experimental import pallas as pl
from jax.experimental.pallas import tpu as pltpu
from jax.sharding import PartitionSpec as P

MESH = pl.DeviceIdType.MESH
HEAD_DIM = 128
RANK = 16
MAPS = 3
HEADS = 32
TOKENS = 128
MEMBERS = 8
CTX = 32
QUERY_BLOCK = 256
GROUP = MEMBERS * TOKENS
adapter_scale = 0.25
SOFTMAX_SCALE = 1.0 / math.sqrt(HEAD_DIM)
LOG2E = 1.4426950408889634
OFFSETS = (1, 3, 2, 4, 5, 7, 6)

HALF = MAPS * RANK // 2
PIECES = 16
PIECE = 128
DEFER = True
VMEM_GRANT = 62 * 1024 * 1024
PAIR_PARTS = 4
PAIR_PIECES = PIECES // PAIR_PARTS

BF = jnp.bfloat16
F32 = jnp.float32
NT = (((1,), (1,)), ((), ()))


def dot(a, b):
    return jnp.dot(a, b, preferred_element_type=F32)


def dot_nt(a, b):
    return lax.dot_general(a, b, NT, preferred_element_type=F32)


def place(me, kind):
    shifted = lax.rem(me + CTX - 4 * kind, CTX)
    position = lax.rem(shifted, MEMBERS)
    return position, shifted - position + 4 * kind


def partner(position, offset):
    half = lax.rem(position // 4 + offset // 4, 2)
    return half * 4 + lax.rem(lax.rem(position, 4) + offset % 4, 4)


def head_positions(mask_ref, visit):
    def step(head, shifted_before):
        flag = mask_ref[head]
        visit(head, jnp.where(flag == 1, HEADS // 2 + shifted_before, head - shifted_before))
        return shifted_before + flag

    lax.fori_loop(0, HEADS, step, jnp.int32(0))


def project_kernel(
    mask_ref, hidden_ref, query_ref, key_ref, value_ref, grad_ref, down_ref, up_ref,
    send_ref, low_ref, own_up_ref, low_rows, perm_ref,
):
    step = pl.program_id(0)
    chunk, half = step // 2, lax.rem(step, 2)
    me = lax.axis_index("ctx")

    @pl.when(step == 0)
    def _():
        def visit(head, position):
            perm_ref[position] = head

        head_positions(mask_ref, visit)
        low_t = dot_nt(down_ref[...], hidden_ref[...])
        low_ref[...] = low_t.astype(BF)
        low_rows[...] = jnp.transpose(low_t).astype(BF)

    def columns_of(place_in_order):
        return pl.ds(pl.multiple_of(perm_ref[place_in_order] * HEAD_DIM, HEAD_DIM), HEAD_DIM)

    low = low_rows[...]
    first = 16 * (chunk // 2) + lax.rem(chunk, 2)
    for i in range(MEMBERS // 2):
        columns = columns_of(first + 2 * (half * (MEMBERS // 2) + i))
        for m, base_ref in enumerate((query_ref, key_ref, value_ref)):
            update = dot(low[:, m * RANK:(m + 1) * RANK], up_ref[m * RANK:(m + 1) * RANK, columns])
            send_ref[0, i, m * TOKENS:(m + 1) * TOKENS, :] = (
                base_ref[:, columns].astype(F32) + adapter_scale * update
            ).astype(BF)
        send_ref[0, i, 3 * TOKENS:4 * TOKENS, :] = grad_ref[:, columns]
    position, _ = place(me, chunk // 2)
    own_up_ref[chunk] = up_ref[:, columns_of(first + 2 * position)]


def restore_kernel(mask_ref, by_order_ref, all_ref, context_ref, grad_down_ref, grad_up_ref, sems):
    def copy(head, position):
        columns = pl.ds(pl.multiple_of(head * HEAD_DIM, HEAD_DIM), HEAD_DIM)
        return pltpu.make_async_copy(by_order_ref.at[position], context_ref.at[:, columns], sems.at[head])

    head_positions(mask_ref, lambda head, position: copy(head, position).start())
    for core in range(2):
        for piece in range(PIECES):
            first = core * PIECES * PIECE + piece * PIECE
            grad_down_ref[:, first:first + PIECE] = all_ref[core, piece, 0].astype(F32)

    def restore(head, position):
        kind, member = position // 16, lax.rem(position, 16) // 2
        parity = jnp.where(kind == 0, member // 4, 1 - member // 4)
        columns = pl.ds(pl.multiple_of(head * HEAD_DIM, HEAD_DIM), HEAD_DIM)
        for part in range(2):
            pieces = all_ref[kind, (2 * lax.rem(position, 2) + part) * 4 + lax.rem(member, 4), 1].astype(F32)
            grad_up_ref[part * HALF:(part + 1) * HALF, columns] = jnp.where(parity == 0, pieces[:HALF], pieces[HALF:])

    head_positions(mask_ref, restore)
    for head in range(HEADS):
        copy(head, 0).wait()


def attention_kernel(
    send_buf, low_own, own_up, hidden_ref,
    ctx_recv, all_buf,
    recv_buf, low_buf, ctx_send, rank_send, rank_recv,
    kt_buf, vt_buf, gt_buf, dqt_buf, dk_buf, dv_buf,
    down_part, down_pair, down_sum, down_recv, up_part, up_pair, up_sum, up_recv, line_buf, up_line_buf,
    send_sem, recv_sem, low_send_sem, low_recv_sem, ctx_send_sem, ctx_recv_sem, rank_send_sem, rank_recv_sem,
    pair_send_sem, pair_recv_sem, plane_send_sem, plane_recv_sem, side_send_sem, side_recv_sem,
    line_send_sem, line_recv_sem, up_line_send_sem, up_line_recv_sem, own_sem, all_send_sem, all_recv_sem, last_send_sem, last_recv_sem,
):
    dp = lax.axis_index("dp")
    me = lax.axis_index("ctx")
    z, x = me // 4, lax.rem(me, 4)
    y, core = dp // 2, lax.rem(dp, 2)
    own_piece = y * 4 + x

    barrier = pltpu.get_barrier_semaphore()
    for dz in (-1, 0, 1):
        for dx in range(4):
            if dz == 0 and dx == 0:
                continue
            peer = lax.rem(z + dz + 8, 8) * 4 + lax.rem(x + dx, 4)
            pl.semaphore_signal(barrier, inc=1, device_id=(dp, peer), device_id_type=MESH)
    for dz in range(2, 7):
        pl.semaphore_signal(barrier, inc=1, device_id=(dp, lax.rem(z + dz, 8) * 4 + x), device_id_type=MESH)
    for dy in range(1, 4):
        for dx in range(4):
            peer = (lax.rem(y + dy, 4) * 2 + core, z * 4 + lax.rem(x + dx, 4))
            pl.semaphore_signal(barrier, inc=1, device_id=peer, device_id_type=MESH)
    sibling = (y * 2 + 1 - core, me)
    pl.semaphore_signal(barrier, inc=1, device_id=sibling, device_id_type=MESH)
    pl.semaphore_wait(barrier, 29)

    def low_copy(kind, offset):
        position, base = place(me, kind)
        target = partner(position, offset)
        return pltpu.make_async_remote_copy(
            src_ref=low_own, dst_ref=low_buf.at[kind, position],
            send_sem=low_send_sem.at[kind, offset], recv_sem=low_recv_sem.at[kind, offset],
            device_id=(dp, lax.rem(base + target, CTX)), device_id_type=MESH,
        )

    def data_copy(chunk, offset):
        position, base = place(me, chunk // 2)
        target = partner(position, offset)
        return pltpu.make_async_remote_copy(
            src_ref=send_buf.at[chunk, target], dst_ref=recv_buf.at[chunk, position],
            send_sem=send_sem.at[chunk, offset], recv_sem=recv_sem.at[chunk, offset],
            device_id=(dp, lax.rem(base + target, CTX)), device_id_type=MESH,
        )

    def context_copy(chunk, offset):
        kind = chunk // 2
        position, base = place(me, kind)
        target = partner(position, offset)
        return pltpu.make_async_remote_copy(
            src_ref=ctx_send.at[chunk, target],
            dst_ref=ctx_recv.at[16 * kind + 2 * position + lax.rem(chunk, 2)],
            send_sem=ctx_send_sem.at[chunk, offset], recv_sem=ctx_recv_sem.at[chunk, offset],
            device_id=(dp, lax.rem(base + target, CTX)), device_id_type=MESH,
        )

    def rank_copy(kind, offset):
        position, base = place(me, kind)
        target = partner(position, offset)
        return pltpu.make_async_remote_copy(
            src_ref=rank_send.at[kind, target], dst_ref=rank_recv.at[kind, offset],
            send_sem=rank_send_sem.at[kind, offset], recv_sem=rank_recv_sem.at[kind, offset],
            device_id=(dp, lax.rem(base + target, CTX)), device_id_type=MESH,
        )

    def own_copy(chunk):
        position, _ = place(me, chunk // 2)
        return pltpu.make_async_copy(
            send_buf.at[chunk, position], recv_buf.at[chunk, position], recv_sem.at[chunk, 0]
        )

    def start(chunk, carry):
        for offset in OFFSETS:
            data_copy(chunk, offset).start()
        own_copy(chunk).start()
        return carry

    start(0, 0)
    for kind in range(2):
        position, _ = place(me, kind)
        low_buf[kind, position] = low_own[...]
        for offset in OFFSETS:
            low_copy(kind, offset).start()
    lax.fori_loop(1, 4, start, 0)
    rank_send[...] = jnp.zeros_like(rank_send)
    for kind in range(2):
        for offset in OFFSETS:
            low_copy(kind, offset).wait_recv()

    def own_context(chunk):
        kind = chunk // 2
        position, _ = place(me, kind)
        return pltpu.make_async_copy(
            ctx_send.at[chunk, position], ctx_recv.at[16 * kind + 2 * position + lax.rem(chunk, 2)], own_sem.at[chunk]
        )

    def send_context(chunk):
        for offset in OFFSETS:
            context_copy(chunk, offset).start()
        own_context(chunk).start()

    def attend(chunk, carry):
        kind = chunk // 2
        for offset in OFFSETS:
            data_copy(chunk, offset).wait_recv()
        own_copy(chunk).wait()
        if DEFER:
            @pl.when(chunk == 3)
            def _():
                lax.fori_loop(0, 3, lambda c, carry: (send_context(c), carry)[1], 0)

        def rows(array, first, count):
            part = recv_buf[chunk, first // TOKENS:(first + count) // TOKENS, array * TOKENS:(array + 1) * TOKENS, :]
            return part.reshape(count, HEAD_DIM)

        kt_buf[...] = jnp.transpose(rows(1, 0, GROUP))
        vt_buf[...] = jnp.transpose(rows(2, 0, GROUP))
        gt_buf[...] = jnp.transpose(rows(3, 0, GROUP))
        for block in reversed(range(GROUP // QUERY_BLOCK)):
            first = block * QUERY_BLOCK
            seen = first + QUERY_BLOCK
            queries = rows(0, first, QUERY_BLOCK)
            grads = rows(3, first, QUERY_BLOCK)
            keys = rows(1, 0, seen)
            values = rows(2, 0, seen)
            scores = dot_nt(keys, queries)
            key_ids = lax.broadcasted_iota(jnp.int32, (seen, QUERY_BLOCK), 0)
            query_ids = lax.broadcasted_iota(jnp.int32, (seen, QUERY_BLOCK), 1) + first
            scores = jnp.where(key_ids <= query_ids, scores, -1e30)
            highest = jnp.max(scores, axis=0, keepdims=True)
            exponent = jnp.exp2((scores - highest) * (SOFTMAX_SCALE * LOG2E))
            weights = exponent * (1.0 / jnp.sum(exponent, axis=0, keepdims=True))
            weights_low = weights.astype(BF)
            attended = dot(vt_buf[:, :seen], weights_low).astype(BF).astype(F32)
            weight_grad = dot_nt(values, grads)
            row_inner = jnp.sum(gt_buf[:, first:seen].astype(F32) * attended, axis=0, keepdims=True)
            score_low = (weights * (weight_grad - row_inner)).astype(BF)
            dqt_buf[:, first:seen] = (dot(kt_buf[:, :seen], score_low) * SOFTMAX_SCALE).astype(BF)
            dk = dot(score_low, queries)
            dv = dot(weights_low, grads)
            if seen == GROUP:
                dk_buf[...] = dk
                dv_buf[...] = dv
            else:
                dk_buf[:seen] += dk
                dv_buf[:seen] += dv
            out_rows = jnp.transpose(attended).astype(BF).reshape(QUERY_BLOCK // TOKENS, TOKENS, HEAD_DIM)
            ctx_send[chunk, first // TOKENS:seen // TOKENS] = out_rows
        if not DEFER:
            send_context(chunk)

        dqt = dqt_buf[...]
        dk = (dk_buf[...] * SOFTMAX_SCALE).astype(BF)
        dv = dv_buf[...].astype(BF)
        low_all = jnp.concatenate([low_buf[kind, s] for s in range(MEMBERS)], axis=1)
        up = own_up[chunk]
        up_grad = adapter_scale * jnp.concatenate(
            [dot_nt(low_all[0:16], dqt), dot(low_all[16:32], dk), dot(low_all[32:48], dv)], axis=0
        )
        up_part[kind, 2 * lax.rem(chunk, 2)] = up_grad[:HALF]
        up_part[kind, 2 * lax.rem(chunk, 2) + 1] = up_grad[HALF:]
        ranks = jnp.concatenate([dot(up[0:16], dqt), dot_nt(up[16:32], dk), dot_nt(up[32:48], dv)], axis=0)
        for s in range(MEMBERS):
            rank_send[kind, s] += ranks[:, s * TOKENS:(s + 1) * TOKENS]

        @pl.when(lax.rem(chunk, 2) == 1)
        def _():
            for offset in OFFSETS:
                rank_copy(kind, offset).start()

        return carry

    lax.fori_loop(0, 4, attend, 0)

    for kind in range(2):
        for offset in OFFSETS:
            rank_copy(kind, offset).wait_recv()
    total = jnp.zeros((MAPS * RANK, TOKENS), F32)
    for kind in range(2):
        position, _ = place(me, kind)
        total += rank_send[kind, position]
        for offset in OFFSETS:
            total += rank_recv[kind, offset]
    total_low = total.astype(BF)

    def pair_copy(part):
        if part == PAIR_PARTS:
            source, target = up_part.at[1 - core], up_pair
        else:
            span = pl.ds(part * PAIR_PIECES, PAIR_PIECES)
            source, target = down_part.at[1 - core, span], down_pair.at[span]
        return pltpu.make_async_remote_copy(
            src_ref=source, dst_ref=target, send_sem=pair_send_sem.at[part], recv_sem=pair_recv_sem.at[part],
            device_id=sibling, device_id_type=MESH,
        )

    def plane_device(offset):
        to_y, to_x = lax.rem(y + offset // 4, 4), lax.rem(x + offset % 4, 4)
        return to_y * 4 + to_x, (to_y * 2 + core, z * 4 + to_x)

    def plane_copy(offset):
        piece, device = plane_device(offset)
        return pltpu.make_async_remote_copy(
            src_ref=down_sum.at[piece], dst_ref=down_recv.at[offset],
            send_sem=plane_send_sem.at[offset], recv_sem=plane_recv_sem.at[offset],
            device_id=device, device_id_type=MESH,
        )

    def side_copy(offset):
        to_y = lax.rem(y + offset, 4)
        return pltpu.make_async_remote_copy(
            src_ref=up_sum.at[to_y], dst_ref=up_recv.at[offset],
            send_sem=side_send_sem.at[offset], recv_sem=side_recv_sem.at[offset],
            device_id=(to_y * 2 + core, me), device_id_type=MESH,
        )

    def line_copy(offset):
        return pltpu.make_async_remote_copy(
            src_ref=line_buf.at[z], dst_ref=line_buf.at[z],
            send_sem=line_send_sem.at[offset], recv_sem=line_recv_sem.at[offset],
            device_id=(dp, lax.rem(z + offset, 8) * 4 + x), device_id_type=MESH,
        )

    def up_line_copy(offset):
        return pltpu.make_async_remote_copy(
            src_ref=up_line_buf.at[z], dst_ref=up_line_buf.at[z],
            send_sem=up_line_send_sem.at[offset], recv_sem=up_line_recv_sem.at[offset],
            device_id=(dp, lax.rem(z + offset, 8) * 4 + x), device_id_type=MESH,
        )

    def all_copy(offset):
        _, device = plane_device(offset)
        return pltpu.make_async_remote_copy(
            src_ref=all_buf.at[core, own_piece], dst_ref=all_buf.at[core, own_piece],
            send_sem=all_send_sem.at[offset], recv_sem=all_recv_sem.at[offset],
            device_id=device, device_id_type=MESH,
        )

    def last_copy(offset):
        piece = lax.rem(y + 4 - offset // 4, 4) * 4 + lax.rem(x + 4 - offset % 4, 4)
        return pltpu.make_async_remote_copy(
            src_ref=all_buf.at[core, piece], dst_ref=all_buf.at[core, piece],
            send_sem=last_send_sem.at[offset], recv_sem=last_recv_sem.at[offset],
            device_id=sibling, device_id_type=MESH,
        )

    pair_copy(PAIR_PARTS).start()
    for part in range(PAIR_PARTS):
        for piece in range(part * PAIR_PIECES, (part + 1) * PAIR_PIECES):
            for half in range(2):
                first = half * PIECES * PIECE + piece * PIECE
                down_part[half, piece] = adapter_scale * dot(total_low, hidden_ref[:, first:first + PIECE])
        pair_copy(part).start()
    pair_copy(PAIR_PARTS).wait_recv()
    up_sum[...] = up_part[core] + up_pair[...]
    for offset in range(1, 4):
        side_copy(offset).start()
    for part in range(PAIR_PARTS):
        pair_copy(part).wait_recv()
    down_sum[...] = (down_part[core] + down_pair[...]).astype(BF)
    for offset in range(1, PIECES):
        plane_copy(offset).start()
    if DEFER:
        send_context(3)

    for offset in range(1, 4):
        side_copy(offset).wait_recv()
    up_line_buf[z] = ((up_sum[y] + up_recv[1]) + up_recv[2]) + up_recv[3]
    for offset in range(1, 8):
        up_line_copy(offset).start()
    reduced = down_part[core, own_piece] + down_pair[own_piece]
    for offset in range(1, PIECES):
        plane_copy(offset).wait_recv()
        reduced = reduced + down_recv[offset].astype(F32)
    line_buf[z] = reduced.astype(BF)
    for offset in range(1, 8):
        line_copy(offset).start()
    for offset in range(1, 8):
        up_line_copy(offset).wait_recv()
    even = (up_line_buf[0] + up_line_buf[2]) + (up_line_buf[4] + up_line_buf[6])
    odd = (up_line_buf[1] + up_line_buf[3]) + (up_line_buf[5] + up_line_buf[7])
    all_buf[core, own_piece, 1] = jnp.concatenate([even, odd], axis=0).astype(BF)
    for offset in range(1, 8):
        line_copy(offset).wait_recv()
    terms = [line_buf[i].astype(F32) for i in range(8)]
    all_buf[core, own_piece, 0] = (
        ((terms[0] + terms[1]) + (terms[2] + terms[3])) + ((terms[4] + terms[5]) + (terms[6] + terms[7]))
    ).astype(BF)
    for offset in range(1, PIECES):
        all_copy(offset).start()
    last_copy(0).start()
    for offset in range(1, PIECES):
        all_copy(offset).wait_recv()
        last_copy(offset).start()
    for offset in range(PIECES):
        last_copy(offset).wait_recv()

    def finish(chunk, carry):
        for offset in OFFSETS:
            context_copy(chunk, offset).wait_recv()
            context_copy(chunk, offset).wait_send()
            data_copy(chunk, offset).wait_send()
        own_context(chunk).wait()
        return carry

    lax.fori_loop(0, 4, finish, 0)
    for kind in range(2):
        for offset in OFFSETS:
            low_copy(kind, offset).wait_send()
            rank_copy(kind, offset).wait_send()
    for part in range(PAIR_PARTS + 1):
        pair_copy(part).wait_send()
    for offset in range(1, 4):
        side_copy(offset).wait_send()
    for offset in range(1, 8):
        line_copy(offset).wait_send()
        up_line_copy(offset).wait_send()
    for offset in range(PIECES):
        last_copy(offset).wait_send()
        if offset:
            plane_copy(offset).wait_send()
            all_copy(offset).wait_send()


def body(hidden, query, key, value, cotangent, down, up, mask):
    width = hidden.shape[2]
    vmem = pl.BlockSpec(memory_space=pltpu.VMEM)
    smem = pl.BlockSpec(memory_space=pltpu.SMEM)
    dma = pltpu.SemaphoreType.DMA
    any_space = pl.BlockSpec(memory_space=pl.ANY)
    whole = pl.BlockSpec((TOKENS, width), lambda i, p: (0, 0))
    maps = pl.BlockSpec((MAPS * RANK, width), lambda i, p: (0, 0))
    send, low_t, own_up = pl.pallas_call(
        project_kernel,
        grid_spec=pltpu.PrefetchScalarGridSpec(
            num_scalar_prefetch=1,
            grid=(8,),
            in_specs=[whole] * 5 + [maps] * 2,
            out_specs=(
                pl.BlockSpec((1, MEMBERS // 2, 4 * TOKENS, HEAD_DIM), lambda i, p: (i // 2, i % 2, 0, 0)),
                pl.BlockSpec((MAPS * RANK, TOKENS), lambda i, p: (0, 0)),
                pl.BlockSpec((4, MAPS * RANK, HEAD_DIM), lambda i, p: (0, 0, 0)),
            ),
            scratch_shapes=[pltpu.VMEM((TOKENS, MAPS * RANK), BF), pltpu.SMEM((HEADS,), jnp.int32)],
        ),
        out_shape=(
            jax.ShapeDtypeStruct((4, MEMBERS, 4 * TOKENS, HEAD_DIM), BF),
            jax.ShapeDtypeStruct((MAPS * RANK, TOKENS), BF),
            jax.ShapeDtypeStruct((4, MAPS * RANK, HEAD_DIM), BF),
        ),
        compiler_params=pltpu.CompilerParams(vmem_limit_bytes=VMEM_GRANT),
        name="project",
    )(
        mask, hidden[0], query[0], key[0], value[0], cotangent[0],
        jnp.transpose(down, (0, 2, 1)).reshape(MAPS * RANK, width), up.reshape(MAPS * RANK, width),
    )
    by_order, summed = pl.pallas_call(
        attention_kernel,
        out_shape=(
            jax.ShapeDtypeStruct((HEADS, TOKENS, HEAD_DIM), BF),
            jax.ShapeDtypeStruct((2, PIECES, 2, MAPS * RANK, HEAD_DIM), BF),
        ),
        in_specs=[any_space, vmem, vmem, vmem],
        out_specs=(any_space, vmem),
        scratch_shapes=[
            pltpu.VMEM((4, MEMBERS, 4 * TOKENS, HEAD_DIM), BF),
            pltpu.VMEM((2, MEMBERS, MAPS * RANK, TOKENS), BF),
            pltpu.VMEM((4, MEMBERS, TOKENS, HEAD_DIM), BF),
            pltpu.VMEM((2, MEMBERS, MAPS * RANK, TOKENS), F32),
            pltpu.VMEM((2, MEMBERS, MAPS * RANK, TOKENS), F32),
            pltpu.VMEM((HEAD_DIM, GROUP), BF),
            pltpu.VMEM((HEAD_DIM, GROUP), BF),
            pltpu.VMEM((HEAD_DIM, GROUP), BF),
            pltpu.VMEM((HEAD_DIM, GROUP), BF),
            pltpu.VMEM((GROUP, HEAD_DIM), F32),
            pltpu.VMEM((GROUP, HEAD_DIM), F32),
            pltpu.VMEM((2, PIECES, MAPS * RANK, PIECE), F32),
            pltpu.VMEM((PIECES, MAPS * RANK, PIECE), F32),
            pltpu.VMEM((PIECES, MAPS * RANK, PIECE), BF),
            pltpu.VMEM((PIECES, MAPS * RANK, PIECE), BF),
            pltpu.VMEM((2, 4, HALF, HEAD_DIM), F32),
            pltpu.VMEM((4, HALF, HEAD_DIM), F32),
            pltpu.VMEM((4, HALF, HEAD_DIM), F32),
            pltpu.VMEM((4, HALF, HEAD_DIM), F32),
            pltpu.VMEM((8, MAPS * RANK, PIECE), BF),
            pltpu.VMEM((8, HALF, HEAD_DIM), F32),
            dma((4, MEMBERS)), dma((4, MEMBERS)), dma((2, MEMBERS)), dma((2, MEMBERS)),
            dma((4, MEMBERS)), dma((4, MEMBERS)), dma((2, MEMBERS)), dma((2, MEMBERS)),
            dma((PAIR_PARTS + 1,)), dma((PAIR_PARTS + 1,)), dma((PIECES,)), dma((PIECES,)), dma((4,)), dma((4,)),
            dma((8,)), dma((8,)), dma((8,)), dma((8,)), dma((4,)), dma((PIECES,)), dma((PIECES,)), dma((PIECES,)), dma((PIECES,)),
        ],
        compiler_params=pltpu.CompilerParams(
            collective_id=0, has_side_effects=True, vmem_limit_bytes=VMEM_GRANT
        ),
        name="shifted_group_attention",
    )(send, low_t, own_up, hidden[0])
    context, grad_down, grad_up = pl.pallas_call(
        restore_kernel,
        out_shape=(
            jax.ShapeDtypeStruct((TOKENS, width), BF),
            jax.ShapeDtypeStruct((MAPS * RANK, width), F32),
            jax.ShapeDtypeStruct((MAPS * RANK, width), F32),
        ),
        in_specs=[smem, any_space, vmem],
        out_specs=(vmem, vmem, vmem),
        scratch_shapes=[dma((HEADS,))],
        compiler_params=pltpu.CompilerParams(vmem_limit_bytes=VMEM_GRANT),
        name="restore_heads",
    )(mask, by_order, summed)
    grad_up = grad_up.reshape(MAPS, RANK, width)
    grad_down = jnp.transpose(grad_down.reshape(MAPS, RANK, width), (0, 2, 1))
    return context[None], grad_down, grad_up


def solution(mesh):
    placed = (P("dp", "ctx", None),) * 5 + (P(),) * 3
    return jax.shard_map(
        body, mesh=mesh, in_specs=placed, out_specs=(P("dp", "ctx", None), P(), P()), check_vma=False
    )
```
